32 devices in a mesh: head: 2 (over y), seq: 16 (over z, x, core).
Axes of the slice: x: 2, y: 2, z: 4, core: 2. Of those that a mesh axis runs over, the one named last changes fastest.
Arguments:
- keys: bfloat16 [65536, 128], P(('head', 'seq')), parts along dimension 0, may hold values from -6 to 6
- values: bfloat16 [65536, 128], P(('head', 'seq')), parts along dimension 0, may hold values from -6 to 6
- queries: bfloat16 [65536, 128], P(('head', 'seq')), parts along dimension 0, may hold values from -160 to 160
- query_positions: int32 [256], P(('head', 'seq')), parts along dimension 0, may hold values from 0 to 32767, as said below
- kept_index: int32 [1024], P('head'), parts along dimension 0, may hold values from 0 to 32767, as said below
- ridge_level: int32 [2], P('head'), parts along dimension 0, may hold values from 20 to 99
Outputs:
- matched_values: float32 [1024, 128], P('head'), parts along dimension 0
- ref_out: float32 [256, 128], P(('head', 'seq')), parts along dimension 0
The draws below stay inside these ranges and needn't reach their ends.
There are 2 independent parts, one for each index of `head`. The reference program is written for one: setup_inputs(seed, part) draws one part's arguments, and reference() takes and returns one part's arrays. A program takes and returns all parts, laid end to end along the dimension named above; each array names one. Nothing has to cross between parts.
Inputs may be any that keep to these rules, and one draw needn't show every extreme that they name: `query_positions`: entries 8 d to 8 (d + 1) - 1 are distinct increasing positions within the slab of positions 2048 d to 2048 (d + 1) - 1. `kept_index`: distinct and increasing.
All inputs are finite; a program needn't handle non-finite values.
Results may differ from the reference program's by a relative error of at most 0.00051.
Values may be sent and summed in bfloat16 or wider, within the bound.
A program may use at most 64 MiB of HBM per device.

```python
import math
import jax
import jax.numpy as jnp
from jax import lax

HD = 128
TOK_DEV = 2048
Q_DEV = 8
KEEP = 512
CACHE = 32768
N_SEQ = 16


def shared_integers(key):
    slab_keys = jax.random.split(jax.random.fold_in(key, 101), N_SEQ)

    def slab_rows(slab_key, slab_number):
        chosen = jax.random.permutation(slab_key, TOK_DEV)[:Q_DEV]
        return jnp.sort(chosen).astype(jnp.int32) + slab_number * TOK_DEV
    slab_numbers = jnp.arange(N_SEQ, dtype=jnp.int32)
    positions = jax.vmap(slab_rows)(slab_keys, slab_numbers).reshape(-1).astype(jnp.int32)
    everyone = jax.random.permutation(jax.random.fold_in(key, 102), TOK_DEV * N_SEQ)
    kept = jnp.sort(everyone[:KEEP]).astype(jnp.int32)
    return (positions, kept)


def shared_floats(key):
    total = TOK_DEV * N_SEQ
    base_keys = jnp.clip(jax.random.normal(jax.random.fold_in(key, 103), (total, HD), jnp.float32), -6.0, 6.0)
    base_queries = jnp.clip(3.0 * jax.random.normal(jax.random.fold_in(key, 104), (total, HD), jnp.float32), -18.0, 18.0)
    return (base_keys, base_queries)


def draw_keys(key, part):
    return shared_floats(key)[0].astype(jnp.bfloat16)


def draw_queries(key, part):
    return shared_floats(key)[1].astype(jnp.bfloat16)


def draw_query_positions(key, part):
    return shared_integers(key)[0]


def draw_kept_index(key, part):
    return shared_integers(key)[1]


def level_of(rng, shape, pieces, least, largest):
    def one(dim, shards_of):
        draws = jax.random.uniform(jax.random.fold_in(jax.random.fold_in(rng, 6), dim), (shards_of,), jnp.float32, least / len(pieces), largest / len(pieces))
        return jnp.repeat(jnp.exp(draws), shape[dim] // shards_of).reshape((-1,) + (1,) * (len(shape) - dim - 1))

    level = one(*pieces[0])
    for cut in pieces[1:]:
        level = level * one(*cut)
    return level


def normal_values(stream_key, extent, width, limit, shards=(), held_as=jnp.bfloat16):
    drawn = width * jax.random.normal(stream_key, extent, jnp.float32)
    if shards:
        drawn = drawn * level_of(stream_key, extent, shards, -0.22, 0.18)
    return jnp.clip(drawn, -limit, limit).astype(held_as)


def setup_inputs(seed: int = 0, part: int = 0) -> dict:
    key_list = jax.random.split(jax.random.key(seed), 7)
    part_keys = jax.random.split(jax.random.fold_in(key_list[6], part), 7)
    keys = draw_keys(jax.random.fold_in(jax.random.fold_in(key_list[6], part), 71), part)
    values = normal_values(part_keys[1], (CACHE, HD), 1.0, 6.0, ((0, 16),))
    queries = draw_queries(jax.random.fold_in(jax.random.fold_in(key_list[6], part), 71), part)
    query_positions = draw_query_positions(jax.random.fold_in(jax.random.fold_in(key_list[6], part), 71), part)
    kept_index = draw_kept_index(jax.random.fold_in(jax.random.fold_in(key_list[6], part), 71), part)
    ridge_level = jax.random.randint(part_keys[5], (1,), 20, 100).astype(jnp.int32)
    return dict(keys=keys, values=values, queries=queries, query_positions=query_positions, kept_index=kept_index, ridge_level=ridge_level)


def slab_partials(query_rows, key_slab, value_slab):
    inv_root = 1.0 / math.sqrt(HD)
    scores = jnp.dot(query_rows.astype(jnp.float32), key_slab.T.astype(jnp.float32), preferred_element_type=jnp.float32) * inv_root
    row_peak = lax.optimization_barrier(jnp.max(scores, axis=1))
    probs = jnp.exp(scores - row_peak[:, None]).astype(jnp.bfloat16)
    totals = lax.optimization_barrier(jnp.sum(probs.astype(jnp.float32), axis=1))
    numer = jnp.dot(probs.astype(jnp.float32), value_slab.astype(jnp.float32), preferred_element_type=jnp.float32)
    return (row_peak, totals, numer)

def reference(keys, values, queries, query_positions, kept_index, ridge_level):
    inv_root = 1.0 / math.sqrt(HD)
    query_rows = jnp.take(queries, query_positions.astype(jnp.int32), axis=0)
    kept_keys = jnp.take(keys, kept_index.astype(jnp.int32), axis=0)
    key_slabs = keys.reshape(N_SEQ, TOK_DEV, HD)
    value_slabs = values.reshape(N_SEQ, TOK_DEV, HD)

    def one_slab(pair):
        return slab_partials(query_rows, pair[0], pair[1])
    maxima, totals, numers = lax.map(one_slab, (key_slabs, value_slabs))
    overall = lax.optimization_barrier(jnp.max(maxima, axis=0))
    factors = jnp.exp(maxima - overall[None, :])
    ref_out = lax.optimization_barrier(jnp.sum(numers * factors[:, :, None], axis=0)) / lax.optimization_barrier(jnp.sum(totals * factors, axis=0))[:, None]
    logits = jnp.dot(query_rows.astype(jnp.float32), kept_keys.T.astype(jnp.float32), preferred_element_type=jnp.float32) * inv_root
    weights = jax.nn.softmax(logits, axis=1)
    gram = jnp.dot(weights.T, weights, precision=lax.Precision.HIGHEST)
    moment = jnp.dot(weights.T, ref_out, precision=lax.Precision.HIGHEST)
    ridge_value = ridge_level[0].astype(jnp.float32) * 0.01
    system = gram + ridge_value * jnp.eye(KEEP, dtype=jnp.float32)
    lower = jnp.linalg.cholesky(system)
    matched_values = jax.scipy.linalg.cho_solve((lower, True), moment)
    return (matched_values, ref_out)
```

```python
import functools
import math

import jax
import jax.numpy as jnp
from jax import lax
from jax.experimental import pallas as pl
from jax.experimental.pallas import tpu as pltpu
from jax.sharding import PartitionSpec as P

MESH = pl.DeviceIdType.MESH
HIGH = lax.Precision.HIGHEST
LANES = 128
SUB = 8


def nt(a, b, precision=None):
    return lax.dot_general(
        a, b, (((1,), (1,)), ((), ())), precision=precision, preferred_element_type=jnp.float32
    )


def inverse_block(m):
    sub = lax.broadcasted_iota(jnp.int32, (SUB, LANES), 0)
    lane = lax.broadcasted_iota(jnp.int32, (SUB, LANES), 1)
    wide_lane = lax.broadcasted_iota(jnp.int32, (LANES, LANES), 1)
    for s in range(0, LANES, SUB):
        rows = m[s : s + SUB, :]
        cols = [jnp.broadcast_to(rows[:, s + j : s + j + 1], (SUB, LANES)) for j in range(SUB)]
        inside = (lane >= s) & (lane < s + SUB)
        work = jnp.where(inside, jnp.where(lane - s == sub, 1.0, 0.0), rows)
        for i in range(SUB):
            here = sub == i
            factor = cols[i]
            pivot = 1.0 / factor[i : i + 1, :]
            for j in range(i + 1, SUB):
                scaled = cols[j][i : i + 1, :] * pivot
                cols[j] = jnp.where(here, scaled, cols[j] - factor * scaled)
            scaled = work[i : i + 1, :] * pivot
            work = jnp.where(here, scaled, work - factor * scaled)
        panel = m[:, s : s + SUB]
        cleared = jnp.where((wide_lane >= s) & (wide_lane < s + SUB), 0.0, m)
        m = cleared - jnp.dot(panel, work, precision=HIGH, preferred_element_type=jnp.float32)
        parts = ([m[:s]] if s else []) + [work] + ([m[s + SUB :]] if s + SUB < LANES else [])
        m = jnp.concatenate(parts, axis=0)
    return m


def invert(s_ref):
    count = s_ref.shape[0]
    if count == LANES:
        s_ref[...] = inverse_block(s_ref[...])
        return

    def turn(k, carry):
        at = pl.ds(pl.multiple_of(k * LANES, LANES), LANES)
        inner = inverse_block(s_ref[at, at])
        s_ref[at, :] = jnp.dot(inner, s_ref[at, :], precision=HIGH, preferred_element_type=jnp.float32)
        s_ref[at, at] = inner

        def row(r, c):
            other = pl.ds(pl.multiple_of(r * LANES, LANES), LANES)

            @pl.when(r != k)
            def _():
                panel = s_ref[other, at]
                s_ref[other, at] = jnp.zeros((LANES, LANES), jnp.float32)
                s_ref[other, :] = s_ref[other, :] - jnp.dot(
                    panel, s_ref[at, :], precision=HIGH, preferred_element_type=jnp.float32
                )

            return c

        return lax.fori_loop(0, count // LANES, row, carry)

    lax.fori_loop(0, count // LANES, turn, 0)


def kernel(
    n,
    pos_ref,
    level_ref,
    kept_ref,
    keys_hbm,
    values_hbm,
    queries_hbm,
    matched_ref,
    ref_ref,
    keys,
    values,
    queries,
    own_q,
    all_q,
    pick,
    pick_in,
    chunk,
    kept_all,
    part,
    part_in,
    own_ref,
    all_ref,
    system,
    load_sem,
    send_sem,
    recv_sem,
):
    me = lax.axis_index("seq")
    slab, head_dim = keys.shape
    own = own_q.shape[0]
    count = n * own
    keep = kept_ref.shape[0] * kept_ref.shape[1]
    each = keep // n
    inv_root = 1.0 / math.sqrt(head_dim)
    start = me * slab

    loads = [
        pltpu.make_async_copy(src, dst, load_sem.at[k])
        for k, (src, dst) in enumerate(((queries_hbm, queries), (keys_hbm, keys), (values_hbm, values)))
    ]
    for load in loads:
        load.start()

    def peer(k):
        return lax.rem(me + k, n)

    barrier = pltpu.get_barrier_semaphore()

    def greet(k, c):
        pl.semaphore_signal(barrier, inc=1, device_id={"seq": peer(k)}, device_id_type=MESH)
        return c

    lax.fori_loop(1, n, greet, 0)

    def copy_of(stage, k, src, dst):
        return pltpu.make_async_remote_copy(
            src_ref=src(peer(k)),
            dst_ref=dst.at[me],
            send_sem=send_sem.at[stage, k],
            recv_sem=recv_sem.at[stage, k],
            device_id={"seq": peer(k)},
            device_id_type=MESH,
        )

    def send(stage, src, dst):
        def one(k, c):
            copy_of(stage, k, src, dst).start()
            return c

        lax.fori_loop(1, n, one, 0)

    def arrive(stage, src, dst):
        def one(k, c):
            copy_of(stage, k, src, dst).wait_recv()
            return c

        lax.fori_loop(1, n, one, 0)

    def sent(stage, src, dst):
        def one(k, c):
            copy_of(stage, k, src, dst).wait_send()
            return c

        lax.fori_loop(1, n, one, 0)

    q_args = (0, lambda p: own_q, all_q)
    pick_args = (1, lambda p: pick.at[p], pick_in)
    kept_args = (2, lambda p: chunk, kept_all)
    part_args = (3, lambda p: part.at[p], part_in)
    ref_args = (4, lambda p: own_ref, all_ref)

    loads[0].wait()
    sub = lax.broadcasted_iota(jnp.int32, (own, slab), 0)
    wanted = jnp.zeros((own, slab), jnp.int32)
    for i in range(own):
        wanted = jnp.where(sub == i, pos_ref[i] - start, wanted)
    chosen = wanted == lax.broadcasted_iota(jnp.int32, (own, slab), 1)
    rows = jnp.dot(
        jnp.where(chosen, 1.0, 0.0).astype(jnp.bfloat16), queries[...], preferred_element_type=jnp.float32
    )
    own_q[...] = rows
    all_q[me] = rows

    loads[1].wait()
    places = lax.broadcasted_iota(jnp.int32, (LANES, slab), 1).astype(jnp.float32)
    for j in range(keep // LANES):
        offset = (kept_ref[j : j + 1, :] - start).astype(jnp.float32)
        offset = jnp.broadcast_to(offset, (LANES, LANES)).T
        chosen = jnp.where(jnp.concatenate([offset] * (slab // LANES), axis=1) == places, 1.0, 0.0)
        found = jnp.dot(chosen.astype(jnp.bfloat16), keys[...], preferred_element_type=jnp.float32)
        pick[pl.ds(j * LANES // each, LANES // each)] = found.astype(pick.dtype).reshape(
            LANES // each, each, head_dim
        )
    pick_in[me] = pick[me]

    pl.semaphore_wait(barrier, n - 1)
    send(*q_args)
    send(*pick_args)
    arrive(*q_args)
    all_queries = all_q[...].reshape(count, head_dim).astype(jnp.bfloat16)
    arrive(*pick_args)
    total = pick_in[0].astype(jnp.float32)
    for k in range(1, n):
        total = total + pick_in[k].astype(jnp.float32)
    chunk[...] = total.astype(chunk.dtype)
    kept_all[me] = total.astype(chunk.dtype)
    send(*kept_args)

    loads[2].wait()
    scores = nt(all_queries, keys[...]) * inv_root
    peak = jnp.max(scores, axis=1, keepdims=True)
    probs = jnp.exp(scores - peak).astype(jnp.bfloat16)
    totals = jnp.sum(probs.astype(jnp.float32), axis=1, keepdims=True)
    numer = jnp.dot(probs, values[...], preferred_element_type=jnp.float32)
    half = lax.broadcasted_iota(jnp.int32, (count, LANES), 1) < LANES // 2
    part[:, :, :head_dim] = numer.reshape(n, own, head_dim)
    part[:, :, head_dim:] = jnp.where(half, peak, totals).reshape(n, own, LANES)
    part_in[me] = part[me]
    send(*part_args)

    arrive(*kept_args)
    kept_keys = kept_all[...].reshape(keep, head_dim).astype(jnp.bfloat16)
    logits = nt(all_queries, kept_keys) * inv_root
    weights = jnp.exp(logits - jnp.max(logits, axis=1, keepdims=True))
    weights = weights / jnp.sum(weights, axis=1, keepdims=True)

    arrive(*part_args)
    stats = part_in[:, :, head_dim:]
    peaks = stats[:, :, 0:1]
    sums = stats[:, :, LANES // 2 : LANES // 2 + 1]
    factors = jnp.exp(peaks - jnp.max(peaks, axis=0, keepdims=True))
    merged = jnp.sum(part_in[:, :, :head_dim] * factors, axis=0) / jnp.sum(sums * factors, axis=0)
    own_ref[...] = merged
    all_ref[me] = merged
    ref_ref[...] = merged
    send(*ref_args)

    ridge = level_ref[0].astype(jnp.float32) * 0.01
    eye = lax.broadcasted_iota(jnp.int32, (count, count), 0) == lax.broadcasted_iota(
        jnp.int32, (count, count), 1
    )
    system[...] = nt(weights, weights, HIGH) + jnp.where(eye, ridge, 0.0)
    invert(system)

    arrive(*ref_args)
    full_ref = all_ref[...].reshape(count, head_dim)
    inner = jnp.dot(system[...], full_ref, precision=HIGH, preferred_element_type=jnp.float32)
    matched_ref[...] = lax.dot_general(
        weights, inner, (((0,), (0,)), ((), ())), precision=HIGH, preferred_element_type=jnp.float32
    )
    for args in (q_args, pick_args, kept_args, part_args, ref_args):
        sent(*args)


def per_device(n, keys, values, queries, query_positions, kept_index, ridge_level):
    slab, head_dim = keys.shape
    own = query_positions.shape[0]
    keep = kept_index.shape[0]
    count = n * own
    each = keep // n
    link = jnp.bfloat16 if each % 16 == 0 else jnp.float32
    vmem = pl.BlockSpec(memory_space=pltpu.VMEM)
    smem = pl.BlockSpec(memory_space=pltpu.SMEM)
    hbm = pl.BlockSpec(memory_space=pl.ANY)
    f32 = jnp.float32
    return pl.pallas_call(
        functools.partial(kernel, n),
        out_shape=(
            jax.ShapeDtypeStruct((keep, head_dim), f32),
            jax.ShapeDtypeStruct((own, head_dim), f32),
        ),
        in_specs=[smem, smem, vmem, hbm, hbm, hbm],
        out_specs=(vmem, vmem),
        scratch_shapes=[
            pltpu.VMEM((slab, head_dim), keys.dtype),
            pltpu.VMEM((slab, head_dim), values.dtype),
            pltpu.VMEM((slab, head_dim), queries.dtype),
            pltpu.VMEM((own, head_dim), f32),
            pltpu.VMEM((n, own, head_dim), f32),
            pltpu.VMEM((n, each, head_dim), link),
            pltpu.VMEM((n, each, head_dim), link),
            pltpu.VMEM((each, head_dim), link),
            pltpu.VMEM((n, each, head_dim), link),
            pltpu.VMEM((n, own, head_dim + LANES), f32),
            pltpu.VMEM((n, own, head_dim + LANES), f32),
            pltpu.VMEM((own, head_dim), f32),
            pltpu.VMEM((n, own, head_dim), f32),
            pltpu.VMEM((count, count), f32),
            pltpu.SemaphoreType.DMA((3,)),
            pltpu.SemaphoreType.DMA((5, n)),
            pltpu.SemaphoreType.DMA((5, n)),
        ],
        compiler_params=pltpu.CompilerParams(
            collective_id=0, has_side_effects=True, vmem_limit_bytes=48 * 1024 * 1024
        ),
    )(
        query_positions,
        ridge_level,
        kept_index.reshape(keep // LANES, LANES),
        keys,
        values,
        queries,
    )


def solution(mesh):
    placed = (
        P(("head", "seq"), None),
        P(("head", "seq"), None),
        P(("head", "seq"), None),
        P(("head", "seq")),
        P("head"),
        P("head"),
    )
    return jax.shard_map(
        functools.partial(per_device, mesh.shape["seq"]),
        mesh=mesh,
        in_specs=placed,
        out_specs=(P("head", None), P(("head", "seq"), None)),
        check_vma=False,
    )
```

```python
import functools
import math

import jax
import jax.numpy as jnp
from jax import lax
from jax.experimental import pallas as pl
from jax.experimental.pallas import tpu as pltpu
from jax.sharding import PartitionSpec as P

MESH = pl.DeviceIdType.MESH
HIGH = lax.Precision.HIGHEST
LANES = 128
SUB = 8


def nt(a, b, precision=None):
    return lax.dot_general(
        a, b, (((1,), (1,)), ((), ())), precision=precision, preferred_element_type=jnp.float32
    )


def inverse_start(m):
    return m, m[:SUB, :]


def inverse_steps(state, first, last):
    m, rows = state
    sub = lax.broadcasted_iota(jnp.int32, (SUB, LANES), 0)
    lane = lax.broadcasted_iota(jnp.int32, (SUB, LANES), 1)
    wide_lane = lax.broadcasted_iota(jnp.int32, (LANES, LANES), 1)
    for s in range(first, last, SUB):
        cols = [jnp.broadcast_to(rows[:, s + j : s + j + 1], (SUB, LANES)) for j in range(SUB)]
        inside = (lane >= s) & (lane < s + SUB)
        work = jnp.where(inside, jnp.where(lane - s == sub, 1.0, 0.0), rows)
        for i in range(SUB):
            here = sub == i
            factor = cols[i]
            pivot = 1.0 / factor[i : i + 1, :]
            for j in range(i + 1, SUB):
                scaled = cols[j][i : i + 1, :] * pivot
                cols[j] = jnp.where(here, scaled, cols[j] - factor * scaled)
            scaled = work[i : i + 1, :] * pivot
            work = jnp.where(here, scaled, work - factor * scaled)
        after = s + SUB
        if after < LANES:
            coming = m[after : after + SUB, :]
            terms = [
                jnp.broadcast_to(coming[:, s + j : s + j + 1], (SUB, LANES)) * work[j : j + 1, :]
                for j in range(SUB)
            ]
            while len(terms) > 1:
                terms = [x + y for x, y in zip(terms[::2], terms[1::2])]
            rows = jnp.where(inside, 0.0, coming) - terms[0]
        panel = m[:, s:after]
        cleared = jnp.where((wide_lane >= s) & (wide_lane < after), 0.0, m)
        m = cleared - jnp.dot(panel, work, precision=HIGH, preferred_element_type=jnp.float32)
        parts = [m[:s]] if s else []
        parts.append(work)
        if after < LANES:
            parts.append(rows)
        if after + SUB < LANES:
            parts.append(m[after + SUB :])
        m = jnp.concatenate(parts, axis=0)
    return m, rows


def inverse_block(m):
    return inverse_steps(inverse_start(m), 0, LANES)[0]


def invert(s_ref):
    count = s_ref.shape[0]
    def turn(k, carry):
        at = pl.ds(pl.multiple_of(k * LANES, LANES), LANES)
        inner = inverse_block(s_ref[at, at])
        s_ref[at, :] = jnp.dot(inner, s_ref[at, :], precision=HIGH, preferred_element_type=jnp.float32)
        s_ref[at, at] = inner

        def row(r, c):
            other = pl.ds(pl.multiple_of(r * LANES, LANES), LANES)

            @pl.when(r != k)
            def _():
                panel = s_ref[other, at]
                s_ref[other, at] = jnp.zeros((LANES, LANES), jnp.float32)
                s_ref[other, :] = s_ref[other, :] - jnp.dot(
                    panel, s_ref[at, :], precision=HIGH, preferred_element_type=jnp.float32
                )

            return c

        return lax.fori_loop(0, count // LANES, row, carry)

    lax.fori_loop(0, count // LANES, turn, 0)


def kernel(
    n,
    pos_hbm,
    level_hbm,
    kept_hbm,
    keys_hbm,
    values_hbm,
    queries_hbm,
    matched_ref,
    ref_ref,
    pos_ref,
    level_ref,
    kept_ref,
    keys,
    values,
    queries,
    own_q,
    all_q,
    pick,
    pick_in,
    chunk,
    kept_all,
    part,
    part_in,
    own_ref,
    all_ref,
    system,
    load_sem,
    send_sem,
    recv_sem,
):
    me = lax.axis_index("seq")
    slab, head_dim = keys.shape
    own = own_q.shape[0]
    count = n * own
    keep = kept_ref.shape[0] * kept_ref.shape[1]
    each = keep // n
    inv_root = 1.0 / math.sqrt(head_dim)
    start = me * slab

    loads = [
        pltpu.make_async_copy(src, dst, load_sem.at[k])
        for k, (src, dst) in enumerate(
            (
                (pos_hbm, pos_ref),
                (queries_hbm, queries),
                (kept_hbm, kept_ref),
                (keys_hbm, keys),
                (values_hbm, values),
                (level_hbm, level_ref),
            )
        )
    ]
    for load in loads:
        load.start()

    def peer(k):
        return lax.rem(me + k, n)

    barrier = pltpu.get_barrier_semaphore()

    def greet(k, c):
        pl.semaphore_signal(barrier, inc=1, device_id={"seq": peer(k)}, device_id_type=MESH)
        return c

    lax.fori_loop(1, n, greet, 0)

    def copy_of(stage, k, src, dst):
        return pltpu.make_async_remote_copy(
            src_ref=src(peer(k)),
            dst_ref=dst.at[me],
            send_sem=send_sem.at[stage, k],
            recv_sem=recv_sem.at[stage, k],
            device_id={"seq": peer(k)},
            device_id_type=MESH,
        )

    def send(stage, src, dst):
        def one(k, c):
            copy_of(stage, k, src, dst).start()
            return c

        lax.fori_loop(1, n, one, 0)

    def arrive(stage, src, dst):
        def one(k, c):
            copy_of(stage, k, src, dst).wait_recv()
            return c

        lax.fori_loop(1, n, one, 0)

    def sent(stage, src, dst):
        def one(k, c):
            copy_of(stage, k, src, dst).wait_send()
            return c

        lax.fori_loop(1, n, one, 0)

    q_args = (0, lambda p: own_q, all_q)
    pick_args = (1, lambda p: pick.at[p], pick_in)
    kept_args = (2, lambda p: chunk, kept_all)
    part_args = (3, lambda p: part.at[p], part_in)
    ref_args = (4, lambda p: own_ref, all_ref)

    loads[0].wait()
    loads[1].wait()
    sub = lax.broadcasted_iota(jnp.int32, (own, slab), 0)
    wanted = jnp.zeros((own, slab), jnp.int32)
    for i in range(own):
        wanted = jnp.where(sub == i, pos_ref[i] - start, wanted)
    chosen = wanted == lax.broadcasted_iota(jnp.int32, (own, slab), 1)
    rows = jnp.dot(
        jnp.where(chosen, 1.0, 0.0).astype(jnp.bfloat16), queries[...], preferred_element_type=jnp.float32
    )
    own_q[...] = rows
    all_q[me] = rows

    loads[2].wait()
    loads[3].wait()
    places = lax.broadcasted_iota(jnp.int32, (LANES, slab), 1).astype(jnp.float32)
    for j in range(keep // LANES):
        offset = (kept_ref[j : j + 1, :] - start).astype(jnp.float32)
        offset = jnp.broadcast_to(offset, (LANES, LANES)).T
        chosen = jnp.where(jnp.concatenate([offset] * (slab // LANES), axis=1) == places, 1.0, 0.0)
        found = jnp.dot(chosen.astype(jnp.bfloat16), keys[...], preferred_element_type=jnp.float32)
        pick[pl.ds(j * LANES // each, LANES // each)] = found.astype(pick.dtype).reshape(
            LANES // each, each, head_dim
        )
    pick_in[me] = pick[me]

    pl.semaphore_wait(barrier, n - 1)
    send(*q_args)
    send(*pick_args)
    arrive(*q_args)
    all_queries = all_q[...].reshape(count, head_dim).astype(jnp.bfloat16)
    arrive(*pick_args)
    total = pick_in[0].astype(jnp.float32)
    for k in range(1, n):
        total = total + pick_in[k].astype(jnp.float32)
    chunk[...] = total.astype(chunk.dtype)
    kept_all[me] = total.astype(chunk.dtype)
    send(*kept_args)

    loads[4].wait()
    scores = nt(all_queries, keys[...]) * inv_root
    peak = jnp.max(scores, axis=1, keepdims=True)
    probs = jnp.exp(scores - peak).astype(jnp.bfloat16)
    totals = jnp.sum(probs.astype(jnp.float32), axis=1, keepdims=True)
    numer = jnp.dot(probs, values[...], preferred_element_type=jnp.float32)
    half = lax.broadcasted_iota(jnp.int32, (count, LANES), 1) < LANES // 2
    part[:, :, :head_dim] = numer.reshape(n, own, head_dim)
    part[:, :, head_dim:] = jnp.where(half, peak, totals).reshape(n, own, LANES)
    part_in[me] = part[me]
    send(*part_args)

    arrive(*kept_args)
    kept_keys = kept_all[...].reshape(keep, head_dim).astype(jnp.bfloat16)
    logits = nt(all_queries, kept_keys) * inv_root
    weights = jnp.exp(logits - jnp.max(logits, axis=1, keepdims=True))
    weights = weights / jnp.sum(weights, axis=1, keepdims=True)

    loads[5].wait()
    ridge = level_ref[0].astype(jnp.float32) * 0.01
    eye = lax.broadcasted_iota(jnp.int32, (count, count), 0) == lax.broadcasted_iota(
        jnp.int32, (count, count), 1
    )
    system[...] = nt(weights, weights, HIGH) + jnp.where(eye, ridge, 0.0)
    single = count == LANES
    if single:
        state = inverse_steps(inverse_start(system[...]), 0, LANES // 2)

    arrive(*part_args)
    stats = part_in[:, :, head_dim:]
    peaks = stats[:, :, 0:1]
    sums = stats[:, :, LANES // 2 : LANES // 2 + 1]
    factors = jnp.exp(peaks - jnp.max(peaks, axis=0, keepdims=True))
    merged = jnp.sum(part_in[:, :, :head_dim] * factors, axis=0) / jnp.sum(sums * factors, axis=0)
    own_ref[...] = merged
    all_ref[me] = merged
    ref_ref[...] = merged
    send(*ref_args)

    if single:
        system[...] = inverse_steps(state, LANES // 2, LANES)[0]
    else:
        invert(system)

    arrive(*ref_args)
    full_ref = all_ref[...].reshape(count, head_dim)
    inner = jnp.dot(system[...], full_ref, precision=HIGH, preferred_element_type=jnp.float32)
    matched_ref[...] = lax.dot_general(
        weights, inner, (((0,), (0,)), ((), ())), precision=HIGH, preferred_element_type=jnp.float32
    )
    for args in (q_args, pick_args, kept_args, part_args, ref_args):
        sent(*args)


def per_device(n, keys, values, queries, query_positions, kept_index, ridge_level):
    slab, head_dim = keys.shape
    own = query_positions.shape[0]
    keep = kept_index.shape[0]
    count = n * own
    each = keep // n
    link = jnp.bfloat16 if each % 16 == 0 else jnp.float32
    vmem = pl.BlockSpec(memory_space=pltpu.VMEM)
    hbm = pl.BlockSpec(memory_space=pltpu.HBM)
    f32 = jnp.float32
    return pl.pallas_call(
        functools.partial(kernel, n),
        out_shape=(
            jax.ShapeDtypeStruct((keep, head_dim), f32),
            jax.ShapeDtypeStruct((own, head_dim), f32),
        ),
        in_specs=[hbm] * 6,
        out_specs=(vmem, vmem),
        scratch_shapes=[
            pltpu.SMEM((own,), jnp.int32),
            pltpu.SMEM((1,), jnp.int32),
            pltpu.VMEM((keep // LANES, LANES), jnp.int32),
            pltpu.VMEM((slab, head_dim), keys.dtype),
            pltpu.VMEM((slab, head_dim), values.dtype),
            pltpu.VMEM((slab, head_dim), queries.dtype),
            pltpu.VMEM((own, head_dim), f32),
            pltpu.VMEM((n, own, head_dim), f32),
            pltpu.VMEM((n, each, head_dim), link),
            pltpu.VMEM((n, each, head_dim), link),
            pltpu.VMEM((each, head_dim), link),
            pltpu.VMEM((n, each, head_dim), link),
            pltpu.VMEM((n, own, head_dim + LANES), f32),
            pltpu.VMEM((n, own, head_dim + LANES), f32),
            pltpu.VMEM((own, head_dim), f32),
            pltpu.VMEM((n, own, head_dim), f32),
            pltpu.VMEM((count, count), f32),
            pltpu.SemaphoreType.DMA((6,)),
            pltpu.SemaphoreType.DMA((5, n)),
            pltpu.SemaphoreType.DMA((5, n)),
        ],
        compiler_params=pltpu.CompilerParams(
            collective_id=0, has_side_effects=True, vmem_limit_bytes=48 * 1024 * 1024
        ),
    )(
        query_positions,
        ridge_level,
        kept_index.reshape(keep // LANES, LANES),
        keys,
        values,
        queries,
    )


def solution(mesh):
    placed = (
        P(("head", "seq"), None),
        P(("head", "seq"), None),
        P(("head", "seq"), None),
        P(("head", "seq")),
        P("head"),
        P("head"),
    )
    return jax.shard_map(
        functools.partial(per_device, mesh.shape["seq"]),
        mesh=mesh,
        in_specs=placed,
        out_specs=(P("head", None), P(("head", "seq"), None)),
        check_vma=False,
    )
```

```python
import functools
import math

import jax
import jax.numpy as jnp
from jax import lax
from jax.experimental import pallas as pl
from jax.experimental.pallas import tpu as pltpu
from jax.sharding import PartitionSpec as P

MESH = pl.DeviceIdType.MESH
HIGH = lax.Precision.HIGHEST
LANES = 128
SUB = 8


def nt(a, b, precision=None):
    return lax.dot_general(
        a, b, (((1,), (1,)), ((), ())), precision=precision, preferred_element_type=jnp.float32
    )


def inverse_start(m):
    return m, m[:SUB, :]


def inverse_steps(state, first, last):
    m, rows = state
    sub = lax.broadcasted_iota(jnp.int32, (SUB, LANES), 0)
    lane = lax.broadcasted_iota(jnp.int32, (SUB, LANES), 1)
    wide_lane = lax.broadcasted_iota(jnp.int32, (LANES, LANES), 1)
    for s in range(first, last, SUB):
        cols = [jnp.broadcast_to(rows[:, s + j : s + j + 1], (SUB, LANES)) for j in range(SUB)]
        inside = (lane >= s) & (lane < s + SUB)
        work = jnp.where(inside, jnp.where(lane - s == sub, 1.0, 0.0), rows)
        for i in range(SUB):
            here = sub == i
            factor = cols[i]
            pivot = 1.0 / factor[i : i + 1, :]
            for j in range(i + 1, SUB):
                scaled = cols[j][i : i + 1, :] * pivot
                cols[j] = jnp.where(here, scaled, cols[j] - factor * scaled)
            scaled = work[i : i + 1, :] * pivot
            work = jnp.where(here, scaled, work - factor * scaled)
        after = s + SUB
        if after < LANES:
            coming = m[after : after + SUB, :]
            terms = [
                jnp.broadcast_to(coming[:, s + j : s + j + 1], (SUB, LANES)) * work[j : j + 1, :]
                for j in range(SUB)
            ]
            while len(terms) > 1:
                terms = [x + y for x, y in zip(terms[::2], terms[1::2])]
            rows = jnp.where(inside, 0.0, coming) - terms[0]
        panel = m[:, s:after]
        cleared = jnp.where((wide_lane >= s) & (wide_lane < after), 0.0, m)
        m = cleared - jnp.dot(panel, work, precision=HIGH, preferred_element_type=jnp.float32)
        parts = [m[:s]] if s else []
        parts.append(work)
        if after < LANES:
            parts.append(rows)
        if after + SUB < LANES:
            parts.append(m[after + SUB :])
        m = jnp.concatenate(parts, axis=0)
    return m, rows


def inverse_block(m):
    return inverse_steps(inverse_start(m), 0, LANES)[0]


def invert(s_ref):
    count = s_ref.shape[0]
    def turn(k, carry):
        at = pl.ds(pl.multiple_of(k * LANES, LANES), LANES)
        inner = inverse_block(s_ref[at, at])
        s_ref[at, :] = jnp.dot(inner, s_ref[at, :], precision=HIGH, preferred_element_type=jnp.float32)
        s_ref[at, at] = inner

        def row(r, c):
            other = pl.ds(pl.multiple_of(r * LANES, LANES), LANES)

            @pl.when(r != k)
            def _():
                panel = s_ref[other, at]
                s_ref[other, at] = jnp.zeros((LANES, LANES), jnp.float32)
                s_ref[other, :] = s_ref[other, :] - jnp.dot(
                    panel, s_ref[at, :], precision=HIGH, preferred_element_type=jnp.float32
                )

            return c

        return lax.fori_loop(0, count // LANES, row, carry)

    lax.fori_loop(0, count // LANES, turn, 0)


def kernel(
    n,
    pos_hbm,
    level_hbm,
    kept_hbm,
    keys_hbm,
    values_hbm,
    queries_hbm,
    matched_ref,
    ref_ref,
    pos_ref,
    level_ref,
    kept_ref,
    keys,
    values,
    queries,
    own_q,
    all_q,
    pick,
    pick_in,
    chunk,
    kept_all,
    part,
    part_in,
    own_ref,
    all_ref,
    system,
    load_sem,
    send_sem,
    recv_sem,
):
    me = lax.axis_index("seq")
    slab, head_dim = keys.shape
    own = own_q.shape[0]
    count = n * own
    keep = kept_ref.shape[0] * kept_ref.shape[1]
    each = keep // n
    inv_root = 1.0 / math.sqrt(head_dim)
    start = me * slab

    loads = [
        pltpu.make_async_copy(src, dst, load_sem.at[k])
        for k, (src, dst) in enumerate(
            (
                (pos_hbm, pos_ref),
                (queries_hbm, queries),
                (kept_hbm, kept_ref),
                (keys_hbm, keys),
                (values_hbm, values),
                (level_hbm, level_ref),
            )
        )
    ]
    for load in loads:
        load.start()

    def peer(k):
        return lax.rem(me + k, n)

    barrier = pltpu.get_barrier_semaphore()

    def greet(k, c):
        pl.semaphore_signal(barrier, inc=1, device_id={"seq": peer(k)}, device_id_type=MESH)
        return c

    lax.fori_loop(1, n, greet, 0)

    def copy_of(stage, k, src, dst):
        return pltpu.make_async_remote_copy(
            src_ref=src(peer(k)),
            dst_ref=dst.at[me],
            send_sem=send_sem.at[stage, k],
            recv_sem=recv_sem.at[stage, k],
            device_id={"seq": peer(k)},
            device_id_type=MESH,
        )

    def send(stage, src, dst):
        def one(k, c):
            copy_of(stage, k, src, dst).start()
            return c

        lax.fori_loop(1, n, one, 0)

    def arrive(stage, src, dst):
        def one(k, c):
            copy_of(stage, k, src, dst).wait_recv()
            return c

        lax.fori_loop(1, n, one, 0)

    def sent(stage, src, dst):
        def one(k, c):
            copy_of(stage, k, src, dst).wait_send()
            return c

        lax.fori_loop(1, n, one, 0)

    q_args = (0, lambda p: own_q, all_q)
    pick_args = (1, lambda p: pick.at[p], pick_in)
    kept_args = (2, lambda p: chunk, kept_all)
    part_args = (3, lambda p: part.at[p], part_in)
    ref_args = (4, lambda p: own_ref, all_ref)

    loads[0].wait()
    loads[1].wait()
    sub = lax.broadcasted_iota(jnp.int32, (own, slab), 0)
    wanted = jnp.zeros((own, slab), jnp.int32)
    for i in range(own):
        wanted = jnp.where(sub == i, pos_ref[i] - start, wanted)
    chosen = wanted == lax.broadcasted_iota(jnp.int32, (own, slab), 1)
    rows = jnp.dot(
        jnp.where(chosen, 1.0, 0.0).astype(jnp.bfloat16), queries[...], preferred_element_type=jnp.float32
    )
    own_q[...] = rows
    all_q[me] = rows

    loads[2].wait()
    loads[3].wait()
    places = lax.broadcasted_iota(jnp.int32, (LANES, slab), 1).astype(jnp.float32)
    for j in range(keep // LANES):
        offset = (kept_ref[j : j + 1, :] - start).astype(jnp.float32)
        offset = jnp.broadcast_to(offset, (LANES, LANES)).T
        chosen = jnp.where(jnp.concatenate([offset] * (slab // LANES), axis=1) == places, 1.0, 0.0)
        found = jnp.dot(chosen.astype(jnp.bfloat16), keys[...], preferred_element_type=jnp.float32)
        pick[pl.ds(j * LANES // each, LANES // each)] = found.astype(pick.dtype).reshape(
            LANES // each, each, head_dim
        )
    pick_in[me] = pick[me]

    pl.semaphore_wait(barrier, n - 1)
    send(*q_args)
    send(*pick_args)
    arrive(*q_args)
    all_queries = all_q[...].reshape(count, head_dim).astype(jnp.bfloat16)
    arrive(*pick_args)
    total = pick_in[0].astype(jnp.float32)
    for k in range(1, n):
        total = total + pick_in[k].astype(jnp.float32)
    chunk[...] = total.astype(chunk.dtype)
    kept_all[me] = total.astype(chunk.dtype)
    send(*kept_args)

    loads[4].wait()
    scores = nt(all_queries, keys[...]) * inv_root
    peak = jnp.max(scores, axis=1, keepdims=True)
    probs = jnp.exp(scores - peak).astype(jnp.bfloat16)
    totals = jnp.sum(probs.astype(jnp.float32), axis=1, keepdims=True)
    numer = jnp.dot(probs, values[...], preferred_element_type=jnp.float32)
    lane = lax.broadcasted_iota(jnp.int32, (n, own, LANES), 2)
    place = lax.broadcasted_iota(jnp.int32, (n, own, LANES), 1)
    stats = jnp.where(lane == place, jnp.broadcast_to(peak, (count, LANES)).reshape(n, own, LANES), 0.0)
    stats = jnp.where(
        lane == place + own, jnp.broadcast_to(totals, (count, LANES)).reshape(n, own, LANES), stats
    )
    part[:, :own, :] = numer.reshape(n, own, head_dim)
    part[:, own:, :] = jnp.sum(stats, axis=1, keepdims=True)
    part_in[me] = part[me]
    send(*part_args)

    arrive(*kept_args)
    kept_keys = kept_all[...].reshape(keep, head_dim).astype(jnp.bfloat16)
    logits = nt(all_queries, kept_keys) * inv_root
    weights = jnp.exp(logits - jnp.max(logits, axis=1, keepdims=True))
    weights = weights / jnp.sum(weights, axis=1, keepdims=True)

    loads[5].wait()
    ridge = level_ref[0].astype(jnp.float32) * 0.01
    eye = lax.broadcasted_iota(jnp.int32, (count, count), 0) == lax.broadcasted_iota(
        jnp.int32, (count, count), 1
    )
    system[...] = nt(weights, weights, HIGH) + jnp.where(eye, ridge, 0.0)
    single = count == LANES
    if single:
        state = inverse_steps(inverse_start(system[...]), 0, LANES // 2)

    arrive(*part_args)
    stats = jnp.broadcast_to(part_in[:, own:, :], (n, own, LANES))
    peaks = jnp.sum(jnp.where(lane == place, stats, 0.0), axis=2, keepdims=True)
    sums = jnp.sum(jnp.where(lane == place + own, stats, 0.0), axis=2, keepdims=True)
    factors = jnp.exp(peaks - jnp.max(peaks, axis=0, keepdims=True))
    merged = jnp.sum(part_in[:, :own, :] * factors, axis=0) / jnp.sum(sums * factors, axis=0)
    own_ref[...] = merged
    all_ref[me] = merged
    ref_ref[...] = merged
    send(*ref_args)

    if single:
        system[...] = inverse_steps(state, LANES // 2, LANES)[0]
    else:
        invert(system)

    arrive(*ref_args)
    full_ref = all_ref[...].reshape(count, head_dim)
    inner = jnp.dot(system[...], full_ref, precision=HIGH, preferred_element_type=jnp.float32)
    matched_ref[...] = lax.dot_general(
        weights, inner, (((0,), (0,)), ((), ())), precision=HIGH, preferred_element_type=jnp.float32
    )
    for args in (q_args, pick_args, kept_args, part_args, ref_args):
        sent(*args)


def per_device(n, keys, values, queries, query_positions, kept_index, ridge_level):
    slab, head_dim = keys.shape
    own = query_positions.shape[0]
    keep = kept_index.shape[0]
    count = n * own
    each = keep // n
    link = jnp.bfloat16 if each % 16 == 0 else jnp.float32
    vmem = pl.BlockSpec(memory_space=pltpu.VMEM)
    hbm = pl.BlockSpec(memory_space=pl.ANY)
    f32 = jnp.float32
    return pl.pallas_call(
        functools.partial(kernel, n),
        out_shape=(
            jax.ShapeDtypeStruct((keep, head_dim), f32),
            jax.ShapeDtypeStruct((own, head_dim), f32),
        ),
        in_specs=[hbm] * 6,
        out_specs=(vmem, vmem),
        scratch_shapes=[
            pltpu.SMEM((own,), jnp.int32),
            pltpu.SMEM((1,), jnp.int32),
            pltpu.VMEM((keep // LANES, LANES), jnp.int32),
            pltpu.VMEM((slab, head_dim), keys.dtype),
            pltpu.VMEM((slab, head_dim), values.dtype),
            pltpu.VMEM((slab, head_dim), queries.dtype),
            pltpu.VMEM((own, head_dim), f32),
            pltpu.VMEM((n, own, head_dim), f32),
            pltpu.VMEM((n, each, head_dim), link),
            pltpu.VMEM((n, each, head_dim), link),
            pltpu.VMEM((each, head_dim), link),
            pltpu.VMEM((n, each, head_dim), link),
            pltpu.VMEM((n, own + 1, head_dim), f32),
            pltpu.VMEM((n, own + 1, head_dim), f32),
            pltpu.VMEM((own, head_dim), f32),
            pltpu.VMEM((n, own, head_dim), f32),
            pltpu.VMEM((count, count), f32),
            pltpu.SemaphoreType.DMA((6,)),
            pltpu.SemaphoreType.DMA((5, n)),
            pltpu.SemaphoreType.DMA((5, n)),
        ],
        compiler_params=pltpu.CompilerParams(
            collective_id=0, has_side_effects=True, vmem_limit_bytes=61000 * 1024
        ),
    )(
        query_positions,
        ridge_level,
        kept_index.reshape(keep // LANES, LANES),
        keys,
        values,
        queries,
    )


def solution(mesh):
    placed = (
        P(("head", "seq"), None),
        P(("head", "seq"), None),
        P(("head", "seq"), None),
        P(("head", "seq")),
        P("head"),
        P("head"),
    )
    return jax.shard_map(
        functools.partial(per_device, mesh.shape["seq"]),
        mesh=mesh,
        in_specs=placed,
        out_specs=(P("head", None), P(("head", "seq"), None)),
        check_vma=False,
    )
```

```python
import functools
import math

import jax
import jax.numpy as jnp
from jax import lax
from jax.experimental import pallas as pl
from jax.experimental.pallas import tpu as pltpu
from jax.sharding import PartitionSpec as P

MESH = pl.DeviceIdType.MESH
HIGH = lax.Precision.HIGHEST
LANES = 128
SUB = 8


def nt(a, b, precision=None):
    return lax.dot_general(
        a, b, (((1,), (1,)), ((), ())), precision=precision, preferred_element_type=jnp.float32
    )


def inverse_start(m):
    return m, m[:SUB, :]


def inverse_steps(state, first, last):
    m, rows = state
    sub = lax.broadcasted_iota(jnp.int32, (SUB, LANES), 0)
    lane = lax.broadcasted_iota(jnp.int32, (SUB, LANES), 1)
    wide_lane = lax.broadcasted_iota(jnp.int32, (LANES, LANES), 1)
    for s in range(first, last, SUB):
        cols = [jnp.broadcast_to(rows[:, s + j : s + j + 1], (SUB, LANES)) for j in range(SUB)]
        inside = (lane >= s) & (lane < s + SUB)
        work = jnp.where(inside, jnp.where(lane - s == sub, 1.0, 0.0), rows)
        for i in range(SUB):
            here = sub == i
            factor = cols[i]
            pivot = 1.0 / factor[i : i + 1, :]
            for j in range(i + 1, SUB):
                scaled = cols[j][i : i + 1, :] * pivot
                cols[j] = jnp.where(here, scaled, cols[j] - factor * scaled)
            scaled = work[i : i + 1, :] * pivot
            work = jnp.where(here, scaled, work - factor * scaled)
        after = s + SUB
        if after < LANES:
            coming = m[after : after + SUB, :]
            terms = [
                jnp.broadcast_to(coming[:, s + j : s + j + 1], (SUB, LANES)) * work[j : j + 1, :]
                for j in range(SUB)
            ]
            while len(terms) > 1:
                terms = [x + y for x, y in zip(terms[::2], terms[1::2])]
            rows = jnp.where(inside, 0.0, coming) - terms[0]
        panel = m[:, s:after]
        cleared = jnp.where((wide_lane >= s) & (wide_lane < after), 0.0, m)
        m = cleared - jnp.dot(panel, work, precision=HIGH, preferred_element_type=jnp.float32)
        parts = [m[:s]] if s else []
        parts.append(work)
        if after < LANES:
            parts.append(rows)
        if after + SUB < LANES:
            parts.append(m[after + SUB :])
        m = jnp.concatenate(parts, axis=0)
    return m, rows


def inverse_block(m):
    return inverse_steps(inverse_start(m), 0, LANES)[0]


def invert(s_ref):
    count = s_ref.shape[0]
    def turn(k, carry):
        at = pl.ds(pl.multiple_of(k * LANES, LANES), LANES)
        inner = inverse_block(s_ref[at, at])
        s_ref[at, :] = jnp.dot(inner, s_ref[at, :], precision=HIGH, preferred_element_type=jnp.float32)
        s_ref[at, at] = inner

        def row(r, c):
            other = pl.ds(pl.multiple_of(r * LANES, LANES), LANES)

            @pl.when(r != k)
            def _():
                panel = s_ref[other, at]
                s_ref[other, at] = jnp.zeros((LANES, LANES), jnp.float32)
                s_ref[other, :] = s_ref[other, :] - jnp.dot(
                    panel, s_ref[at, :], precision=HIGH, preferred_element_type=jnp.float32
                )

            return c

        return lax.fori_loop(0, count // LANES, row, carry)

    lax.fori_loop(0, count // LANES, turn, 0)


def kernel(
    n,
    pos_hbm,
    level_hbm,
    kept_hbm,
    keys_hbm,
    values_hbm,
    queries_hbm,
    matched_ref,
    ref_ref,
    pos_ref,
    level_ref,
    kept_ref,
    keys,
    values,
    queries,
    own_q,
    all_q,
    pick,
    pick_in,
    chunk,
    kept_all,
    part,
    part_in,
    own_ref,
    all_ref,
    system,
    load_sem,
    send_sem,
    recv_sem,
):
    me = lax.axis_index("seq")
    slab, head_dim = keys.shape
    own = own_q.shape[0]
    count = n * own
    keep = kept_ref.shape[0] * kept_ref.shape[1]
    each = keep // n
    inv_root = 1.0 / math.sqrt(head_dim)
    start = me * slab

    loads = [
        pltpu.make_async_copy(src, dst, load_sem.at[k])
        for k, (src, dst) in enumerate(
            (
                (pos_hbm, pos_ref),
                (queries_hbm, queries),
                (kept_hbm, kept_ref),
                (keys_hbm, keys),
                (values_hbm, values),
                (level_hbm, level_ref),
            )
        )
    ]
    for load in loads:
        load.start()

    def peer(k):
        return lax.rem(me + k, n)

    barrier = pltpu.get_barrier_semaphore()

    def greet(k, c):
        pl.semaphore_signal(barrier, inc=1, device_id={"seq": peer(k)}, device_id_type=MESH)
        return c

    lax.fori_loop(1, n, greet, 0)

    def copy_of(stage, k, src, dst):
        return pltpu.make_async_remote_copy(
            src_ref=src(peer(k)),
            dst_ref=dst.at[me],
            send_sem=send_sem.at[stage, k],
            recv_sem=recv_sem.at[stage, k],
            device_id={"seq": peer(k)},
            device_id_type=MESH,
        )

    def send(stage, src, dst):
        def one(j, c):
            k = n // 2 + (j + 1) // 2 * (1 - j % 2 * 2)
            copy_of(stage, k, src, dst).start()
            return c

        lax.fori_loop(0, n - 1, one, 0)

    def arrive(stage, src, dst):
        def one(k, c):
            copy_of(stage, k, src, dst).wait_recv()
            return c

        lax.fori_loop(1, n, one, 0)

    def sent(stage, src, dst):
        def one(k, c):
            copy_of(stage, k, src, dst).wait_send()
            return c

        lax.fori_loop(1, n, one, 0)

    q_args = (0, lambda p: own_q, all_q)
    pick_args = (1, lambda p: pick.at[p], pick_in)
    kept_args = (2, lambda p: chunk, kept_all)
    part_args = (3, lambda p: part.at[p], part_in)
    ref_args = (4, lambda p: own_ref, all_ref)

    loads[0].wait()
    loads[1].wait()
    sub = lax.broadcasted_iota(jnp.int32, (own, slab), 0)
    wanted = jnp.zeros((own, slab), jnp.int32)
    for i in range(own):
        wanted = jnp.where(sub == i, pos_ref[i] - start, wanted)
    chosen = wanted == lax.broadcasted_iota(jnp.int32, (own, slab), 1)
    rows = jnp.dot(
        jnp.where(chosen, 1.0, 0.0).astype(jnp.bfloat16), queries[...], preferred_element_type=jnp.float32
    )
    own_q[...] = rows
    all_q[me] = rows

    loads[2].wait()
    loads[3].wait()
    places = lax.broadcasted_iota(jnp.int32, (LANES, slab), 1).astype(jnp.float32)
    for j in range(keep // LANES):
        offset = (kept_ref[j : j + 1, :] - start).astype(jnp.float32)
        offset = jnp.broadcast_to(offset, (LANES, LANES)).T
        chosen = jnp.where(jnp.concatenate([offset] * (slab // LANES), axis=1) == places, 1.0, 0.0)
        found = jnp.dot(chosen.astype(jnp.bfloat16), keys[...], preferred_element_type=jnp.float32)
        pick[pl.ds(j * LANES // each, LANES // each)] = found.astype(pick.dtype).reshape(
            LANES // each, each, head_dim
        )
    pick_in[me] = pick[me]

    pl.semaphore_wait(barrier, n - 1)
    send(*pick_args)
    send(*q_args)
    arrive(*pick_args)
    total = pick_in[0].astype(jnp.float32)
    for k in range(1, n):
        total = total + pick_in[k].astype(jnp.float32)
    chunk[...] = total.astype(chunk.dtype)
    kept_all[me] = total.astype(chunk.dtype)
    send(*kept_args)

    arrive(*q_args)
    all_queries = all_q[...].reshape(count, head_dim).astype(jnp.bfloat16)
    loads[4].wait()
    scores = nt(all_queries, keys[...]) * inv_root
    peak = jnp.max(scores, axis=1, keepdims=True)
    probs = jnp.exp(scores - peak).astype(jnp.bfloat16)
    totals = jnp.sum(probs.astype(jnp.float32), axis=1, keepdims=True)
    numer = jnp.dot(probs, values[...], preferred_element_type=jnp.float32)
    lane = lax.broadcasted_iota(jnp.int32, (n, own, LANES), 2)
    place = lax.broadcasted_iota(jnp.int32, (n, own, LANES), 1)
    stats = jnp.where(lane == place, jnp.broadcast_to(peak, (count, LANES)).reshape(n, own, LANES), 0.0)
    stats = jnp.where(
        lane == place + own, jnp.broadcast_to(totals, (count, LANES)).reshape(n, own, LANES), stats
    )
    part[:, :own, :] = numer.reshape(n, own, head_dim)
    part[:, own:, :] = jnp.sum(stats, axis=1, keepdims=True)
    part_in[me] = part[me]
    send(*part_args)

    arrive(*kept_args)
    kept_keys = kept_all[...].reshape(keep, head_dim).astype(jnp.bfloat16)
    logits = nt(all_queries, kept_keys) * inv_root
    weights = jnp.exp(logits - jnp.max(logits, axis=1, keepdims=True))
    weights = weights / jnp.sum(weights, axis=1, keepdims=True)

    loads[5].wait()
    ridge = level_ref[0].astype(jnp.float32) * 0.01
    eye = lax.broadcasted_iota(jnp.int32, (count, count), 0) == lax.broadcasted_iota(
        jnp.int32, (count, count), 1
    )
    system[...] = nt(weights, weights, HIGH) + jnp.where(eye, ridge, 0.0)
    single = count == LANES
    if single:
        state = inverse_steps(inverse_start(system[...]), 0, LANES // 2)

    arrive(*part_args)
    stats = jnp.broadcast_to(part_in[:, own:, :], (n, own, LANES))
    peaks = jnp.sum(jnp.where(lane == place, stats, 0.0), axis=2, keepdims=True)
    sums = jnp.sum(jnp.where(lane == place + own, stats, 0.0), axis=2, keepdims=True)
    factors = jnp.exp(peaks - jnp.max(peaks, axis=0, keepdims=True))
    merged = jnp.sum(part_in[:, :own, :] * factors, axis=0) / jnp.sum(sums * factors, axis=0)
    own_ref[...] = merged
    all_ref[me] = merged
    ref_ref[...] = merged
    send(*ref_args)

    if single:
        system[...] = inverse_steps(state, LANES // 2, LANES)[0]
    else:
        invert(system)

    arrive(*ref_args)
    full_ref = all_ref[...].reshape(count, head_dim)
    inner = jnp.dot(system[...], full_ref, precision=HIGH, preferred_element_type=jnp.float32)
    matched_ref[...] = lax.dot_general(
        weights, inner, (((0,), (0,)), ((), ())), precision=HIGH, preferred_element_type=jnp.float32
    )
    for args in (q_args, pick_args, kept_args, part_args, ref_args):
        sent(*args)


def per_device(n, keys, values, queries, query_positions, kept_index, ridge_level):
    slab, head_dim = keys.shape
    own = query_positions.shape[0]
    keep = kept_index.shape[0]
    count = n * own
    each = keep // n
    link = jnp.bfloat16 if each % 16 == 0 else jnp.float32
    vmem = pl.BlockSpec(memory_space=pltpu.VMEM)
    hbm = pl.BlockSpec(memory_space=pl.ANY)
    f32 = jnp.float32
    return pl.pallas_call(
        functools.partial(kernel, n),
        out_shape=(
            jax.ShapeDtypeStruct((keep, head_dim), f32),
            jax.ShapeDtypeStruct((own, head_dim), f32),
        ),
        in_specs=[hbm] * 6,
        out_specs=(vmem, vmem),
        scratch_shapes=[
            pltpu.SMEM((own,), jnp.int32),
            pltpu.SMEM((1,), jnp.int32),
            pltpu.VMEM((keep // LANES, LANES), jnp.int32),
            pltpu.VMEM((slab, head_dim), keys.dtype),
            pltpu.VMEM((slab, head_dim), values.dtype),
            pltpu.VMEM((slab, head_dim), queries.dtype),
            pltpu.VMEM((own, head_dim), f32),
            pltpu.VMEM((n, own, head_dim), f32),
            pltpu.VMEM((n, each, head_dim), link),
            pltpu.VMEM((n, each, head_dim), link),
            pltpu.VMEM((each, head_dim), link),
            pltpu.VMEM((n, each, head_dim), link),
            pltpu.VMEM((n, own + 1, head_dim), f32),
            pltpu.VMEM((n, own + 1, head_dim), f32),
            pltpu.VMEM((own, head_dim), f32),
            pltpu.VMEM((n, own, head_dim), f32),
            pltpu.VMEM((count, count), f32),
            pltpu.SemaphoreType.DMA((6,)),
            pltpu.SemaphoreType.DMA((5, n)),
            pltpu.SemaphoreType.DMA((5, n)),
        ],
        compiler_params=pltpu.CompilerParams(
            collective_id=0, has_side_effects=True, vmem_limit_bytes=61000 * 1024
        ),
    )(
        query_positions,
        ridge_level,
        kept_index.reshape(keep // LANES, LANES),
        keys,
        values,
        queries,
    )


def solution(mesh):
    placed = (
        P(("head", "seq"), None),
        P(("head", "seq"), None),
        P(("head", "seq"), None),
        P(("head", "seq")),
        P("head"),
        P("head"),
    )
    return jax.shard_map(
        functools.partial(per_device, mesh.shape["seq"]),
        mesh=mesh,
        in_specs=placed,
        out_specs=(P("head", None), P(("head", "seq"), None)),
        check_vma=False,
    )
```
